32 devices in a mesh: groups: 2 (over x), row: 16 (over z, y, core).
Axes of the slice: x: 2, y: 2, z: 4, core: 2. Of those that a mesh axis runs over, the one named last changes fastest.
Arguments:
- pair_rows: bfloat16 [256, 128, 128], P(('groups', 'row')), parts along dimension 0, may hold values from -6 to 6
- in_gain: float32 [128], replicated, may hold values from 0.1 to 1.9
- w_left: bfloat16 [128, 128], replicated, may hold values from -0.5 to 0.5
- w_left_gate: bfloat16 [128, 128], replicated, may hold values from -0.5 to 0.5
- w_right: bfloat16 [128, 128], replicated, may hold values from -0.5 to 0.5
- w_right_gate: bfloat16 [128, 128], replicated, may hold values from -0.5 to 0.5
- w_gate: bfloat16 [128, 128], replicated, may hold values from -0.5 to 0.5
- w_out: bfloat16 [128, 128], replicated, may hold values from -0.5 to 0.5
- out_gain: float32 [128], replicated, may hold values from 0.1 to 1.9
- valid_len: int32 [2], P('groups'), parts along dimension 0, may hold values from 64 to 128
- window: int32 [2], P('groups'), parts along dimension 0, may hold values from 0 to 7
Outputs:
- update: bfloat16 [256, 16, 128], P(('groups', 'row')), parts along dimension 0
The draws below stay inside these ranges and needn't reach their ends.
There are 2 independent parts, one for each index of `groups`. The reference program is written for one: setup_inputs(seed, part) draws one part's arguments, and reference() takes and returns one part's arrays. A program takes and returns all parts, laid end to end along the dimension named above; an argument that names none is the same for every part. Nothing has to cross between parts.
All inputs are finite; a program needn't handle non-finite values.
Results may differ from the reference program's by a relative error of at most 0.0078.
Values may be sent and summed in bfloat16 or wider, within the bound.
A program may use at most 128 MiB of HBM per device.

```python
import jax
import jax.numpy as jnp
from jax import lax

C = 128
TOKENS = 128


def steps_of(key, shape, shards, smallest, high):
    loudness, own = 1.0, jax.random.fold_in(key, 6)
    for axis_at, shards_of in shards:
        heights = jnp.exp(jax.random.uniform(jax.random.fold_in(own, axis_at), (shards_of,), jnp.float32, smallest / len(shards), high / len(shards)))
        loudness = loudness * jnp.repeat(heights, shape[axis_at] // shards_of).reshape([-1 if axis == axis_at else 1 for axis in range(len(shape))])
    return loudness


def scatter_about(own_key, shape, deviation, most, shards=(), kind=jnp.bfloat16):
    drawn = jax.random.normal(own_key, shape, jnp.float32) * deviation
    if len(shards) > 0:
        drawn = steps_of(own_key, shape, shards, -0.22, 0.18) * drawn
    return jnp.clip(drawn, min=-most, max=most).astype(kind)


def setup_inputs(seed: int = 0, part: int = 0) -> dict:
    seeds = jax.random.split(jax.random.key(seed), 12)
    part_splits = jax.random.split(jax.random.fold_in(seeds[11], part), 12)
    return {
        "pair_rows": scatter_about(part_splits[0], (TOKENS, TOKENS, C), 1.0, 6.0, ((0, 16),)),
        "in_gain": jnp.clip(1.0 + 0.18 * jax.random.normal(seeds[1], (C,), jnp.float32), 0.1, 1.9),
        "w_left": scatter_about(seeds[2], (C, C), C ** -0.5, 0.5),
        "w_left_gate": scatter_about(seeds[3], (C, C), C ** -0.5, 0.5),
        "w_right": scatter_about(seeds[4], (C, C), C ** -0.5, 0.5),
        "w_right_gate": scatter_about(seeds[5], (C, C), C ** -0.5, 0.5),
        "w_gate": scatter_about(seeds[6], (C, C), C ** -0.5, 0.5),
        "w_out": scatter_about(seeds[7], (C, C), C ** -0.5, 0.5),
        "out_gain": jnp.clip(1.0 + 0.18 * jax.random.normal(seeds[8], (C,), jnp.float32), 0.1, 1.9),
        "valid_len": jax.random.randint(part_splits[9], (1,), TOKENS // 2, TOKENS + 1).astype(jnp.int32),
        "window": jax.random.randint(part_splits[10], (1,), 0, 8).astype(jnp.int32),
    }


def layer_norm(values, gain):
    mean_v = lax.optimization_barrier(jnp.mean(values, axis=-1, keepdims=True))
    centered = values - mean_v
    variance_v = lax.optimization_barrier(jnp.mean(centered * centered, axis=-1, keepdims=True))
    return centered * lax.rsqrt(variance_v + 1e-05) * gain

def edge_of(normed_rows, w_value, w_gating, mask_rows):
    channels = normed_rows.shape[-1]
    flat_rows = normed_rows.reshape(-1, channels)
    value_part = jnp.dot(flat_rows, w_value, preferred_element_type=jnp.float32)
    gating = jnp.dot(flat_rows, w_gating, preferred_element_type=jnp.float32)
    return ((jax.nn.sigmoid(gating) * value_part).reshape(normed_rows.shape) * mask_rows).astype(jnp.bfloat16)

def reference(pair_rows, in_gain, w_left, w_left_gate, w_right, w_right_gate, w_gate, w_out, out_gain, valid_len, window):
    tokens_all = pair_rows.shape[0]
    channels = pair_rows.shape[2]
    width_win = tokens_all // 8
    normed = layer_norm(pair_rows.astype(jnp.float32), in_gain).astype(jnp.bfloat16)
    col_live = (jnp.arange(tokens_all, dtype=jnp.int32) < valid_len[0]).astype(jnp.float32)
    live_mask = (col_live[:, None] * col_live[None, :])[:, :, None]
    start_row = (window[0] * width_win).astype(jnp.int32)
    left_edge = edge_of(normed, w_left, w_left_gate, live_mask)
    win_rows = lax.dynamic_slice_in_dim(normed, start_row, width_win, 0)
    win_mask = lax.dynamic_slice_in_dim(live_mask, start_row, width_win, 0)
    right_edge = edge_of(win_rows, w_right, w_right_gate, win_mask)
    gate_in = lax.dynamic_slice_in_dim(normed, start_row, width_win, 1)
    gate_vals = jax.nn.sigmoid(jnp.dot(gate_in.reshape(-1, channels), w_gate, preferred_element_type=jnp.float32))
    gate_vals = gate_vals.reshape(tokens_all, width_win, channels)
    product = jnp.einsum('ikc,jkc->ijc', left_edge.astype(jnp.float32), right_edge.astype(jnp.float32))
    normed_out = layer_norm(product, out_gain).astype(jnp.bfloat16)
    projected = jnp.dot(normed_out.reshape(-1, channels), w_out, preferred_element_type=jnp.float32)
    return (gate_vals * projected.reshape(tokens_all, width_win, channels)).astype(jnp.bfloat16)
```

```python
import functools

import jax
import jax.numpy as jnp
from jax import lax
from jax.experimental import pallas as pl
from jax.experimental.pallas import tpu as pltpu
from jax.sharding import PartitionSpec as P


def layer_norm(values, gain):
    mean_v = jnp.mean(values, axis=-1, keepdims=True)
    centered = values - mean_v
    variance_v = jnp.mean(centered * centered, axis=-1, keepdims=True)
    return centered * lax.rsqrt(variance_v + 1e-05) * gain


def on_device(
    pair_rows,
    in_gain,
    w_left,
    w_left_gate,
    w_right,
    w_right_gate,
    w_gate,
    w_out,
    out_gain,
    valid_len,
    window,
):
    my_index = lax.axis_index("row")
    local_rows, tokens_all, channels = pair_rows.shape
    width_win = tokens_all // 8
    valid_upto = valid_len[0]
    start_block = window[0]
    start_row = start_block * width_win
    row_ids = my_index * local_rows + jnp.arange(local_rows, dtype=jnp.int32)
    row_live = (row_ids < valid_upto).astype(jnp.float32)
    col_live = (jnp.arange(tokens_all, dtype=jnp.int32) < valid_upto).astype(jnp.float32)
    live_mask = (row_live[:, None] * col_live[None, :])[:, :, None]
    normed = layer_norm(pair_rows.astype(jnp.float32), in_gain).astype(jnp.bfloat16)
    flat_rows = normed.reshape(-1, channels)
    joined = jnp.concatenate([w_left, w_left_gate, w_right, w_right_gate], axis=1)
    projected = jnp.dot(flat_rows, joined, preferred_element_type=jnp.float32)
    projected = projected.reshape(local_rows, tokens_all, 4 * channels)
    left_edge = (
        jax.nn.sigmoid(projected[:, :, channels : 2 * channels])
        * projected[:, :, :channels]
        * live_mask
    ).astype(jnp.bfloat16)
    right_edge = (
        jax.nn.sigmoid(projected[:, :, 3 * channels :])
        * projected[:, :, 2 * channels : 3 * channels]
        * live_mask
    ).astype(jnp.bfloat16)
    gate_in = lax.dynamic_slice_in_dim(normed, start_row, width_win, 1)
    gate_vals = jax.nn.sigmoid(
        jnp.dot(gate_in.reshape(-1, channels), w_gate, preferred_element_type=jnp.float32)
    )
    gate_vals = gate_vals.reshape(local_rows, width_win, channels)
    regrouped = lax.all_to_all(right_edge, "row", split_axis=1, concat_axis=0, tiled=True)
    picked = lax.dynamic_slice_in_dim(regrouped, start_row, width_win, 0)
    window_right = lax.all_gather(picked, "row", axis=1, tiled=True)
    product = jnp.einsum(
        "ikc,jkc->ijc", left_edge, window_right, preferred_element_type=jnp.float32
    )
    normed_out = layer_norm(product, out_gain).astype(jnp.bfloat16)
    result = jnp.dot(normed_out.reshape(-1, channels), w_out, preferred_element_type=jnp.float32)
    return (gate_vals * result.reshape(local_rows, width_win, channels)).astype(jnp.bfloat16)


MESH = pl.DeviceIdType.MESH
CHUNKS = 2
QUAD = 4
PEERS = 3
HOME = PEERS
QUARTER, CROSS, FORWARD, PARTIAL = 0, PEERS, PEERS + 1, 2 * PEERS + 2


def fused_kernel(
    valid_hbm,
    window_hbm,
    x_hbm,
    in_gain_hbm,
    w_left_hbm,
    w_left_gate_hbm,
    w_right_hbm,
    w_right_gate_hbm,
    w_gate_hbm,
    w_out_hbm,
    out_gain_hbm,
    o_ref,
    valid_ref,
    window_ref,
    x_ref,
    in_gain_ref,
    w_l_ref,
    w_r_ref,
    w_gate_ref,
    w_out_ref,
    out_gain_ref,
    parts,
    best,
    cross,
    left_ref,
    right_ref,
    outbox,
    inbox,
    send_sem,
    recv_sem,
    load_sem,
):
    local_rows, tokens, channels = x_ref.shape
    depth = tokens // QUAD
    width = o_ref.shape[1]
    step = local_rows // CHUNKS

    me = lax.axis_index("row")
    core = lax.rem(me, 2)
    chip = lax.div(me, 2)
    quad = lax.div(chip, QUAD)
    spot = lax.rem(chip, QUAD)
    y = lax.rem(spot, 2)
    z = lax.div(spot, 2)
    spots = ((1 - z) * 2 + 1 - y, (1 - z) * 2 + y, z * 2 + 1 - y, spot)

    def at(quad_, spot_, core_):
        return {"row": (quad_ * QUAD + spot_) * 2 + core_}

    cores = (core, 1 - core)
    cross_peer = at(1 - quad, spot, core)
    partner = at(quad, spot, 1 - core)

    def quarter(s):
        return pl.ds(pl.multiple_of(s * depth, depth), depth)

    mine = quarter(spot)

    def remote(src, dst, kind, q, dev):
        return pltpu.make_async_remote_copy(
            src_ref=src,
            dst_ref=dst,
            send_sem=send_sem.at[kind, q],
            recv_sem=recv_sem.at[kind, q],
            device_id=dev,
            device_id_type=MESH,
        )

    def quarter_copy(t, q):
        rows = pl.ds(q * step, step)
        return remote(x_hbm.at[rows, quarter(spots[t])], parts.at[t, 0, rows], QUARTER + t, q, at(quad, spots[t], core))

    def cross_copy(q):
        rows = pl.ds(q * step, step)
        return remote(best.at[rows], cross.at[rows], CROSS, q, cross_peer)

    def forward_copy(t):
        src = x_hbm.at[:, mine] if t == HOME else parts.at[t, 0]
        return remote(src, parts.at[t, 1], FORWARD + t, 0, partner)

    def partial_copy(t, k):
        return remote(outbox.at[t, k], inbox.at[t, k], PARTIAL + t, k, at(quad, spots[t], cores[k]))

    barrier = pltpu.get_barrier_semaphore()
    everyone = [cross_peer] + [at(quad, s, c) for s in spots for c in cores][:-2] + [partner]
    for peer in everyone:
        pl.semaphore_signal(barrier, inc=1, device_id=peer, device_id_type=MESH)
    half = pl.ds(0, channels)
    other = pl.ds(channels, channels)
    loads = [
        pltpu.make_async_copy(src, dst, load_sem.at[n])
        for n, (src, dst) in enumerate(
            (
                (x_hbm.at[:, mine], parts.at[HOME, 0]),
                (valid_hbm, valid_ref),
                (window_hbm, window_ref),
                (in_gain_hbm, in_gain_ref),
                (w_left_hbm, w_l_ref.at[:, half]),
                (w_left_gate_hbm, w_l_ref.at[:, other]),
                (x_hbm, x_ref),
                (w_gate_hbm, w_gate_ref),
                (w_right_hbm, w_r_ref.at[:, half]),
                (w_right_gate_hbm, w_r_ref.at[:, other]),
                (w_out_hbm, w_out_ref),
                (out_gain_hbm, out_gain_ref),
            )
        )
    ]
    for load in loads:
        load.start()
    pl.semaphore_wait(barrier, len(everyone))
    for q in range(CHUNKS):
        for t in range(PEERS):
            quarter_copy(t, q).start()
    forward_copy(HOME).start()
    for load in loads:
        load.wait()

    win = window_ref[0, 0]
    valid = valid_ref[0, 0]
    win_v = jnp.full((depth, channels), win, jnp.int32)

    def flag(cond):
        return jnp.where(cond, 1.0, 0.0).astype(jnp.bfloat16)

    owners = [flag(win_v == quad * QUAD + s) for s in spots[:PEERS]]
    own_quad = flag(jnp.logical_and(win_v >= quad * QUAD, win_v < (quad + 1) * QUAD))

    def pick(own, a, b):
        return jnp.where((own > 0)[None], a, b)

    gain = in_gain_ref[...]
    k_ids = spot * depth + lax.broadcasted_iota(jnp.int32, (depth, channels), 0)
    valid_v = jnp.full((depth, channels), valid, jnp.int32)
    k_live = k_ids < valid_v

    def normal(rows):
        flat = rows.astype(jnp.float32).reshape(-1, channels)
        return layer_norm(flat, gain).astype(jnp.bfloat16)

    def edge(rows, weights, first):
        count = rows.shape[0]
        proj = jnp.dot(normal(rows), weights, preferred_element_type=jnp.float32)
        val = jax.nn.sigmoid(proj[:, channels:]) * proj[:, :channels]
        val = val.reshape(count, depth, channels)
        row_v = jnp.full((depth, channels), first, jnp.int32)
        out = []
        for r in range(count):
            live = jnp.logical_and(k_live, row_v + r < valid_v)
            rounded = jnp.where(live, val[r], 0.0).astype(jnp.bfloat16)
            out.append(rounded.astype(jnp.float32))
        return out

    def left(t, k):
        first = ((quad * QUAD + spots[t]) * 2 + cores[k]) * local_rows
        for r, e in enumerate(edge(parts[t, k], w_l_ref[...], first)):
            left_ref[t, k, r] = e

    gate_in = x_ref[:, :width, :]
    for block in range(1, tokens // width):
        at_block = flag(win_v[:width] == block)
        gate_in = pick(at_block, x_ref[:, block * width : (block + 1) * width, :], gate_in)
    gate_in = normal(gate_in)
    gate_vals = jax.nn.sigmoid(
        jnp.dot(gate_in, w_gate_ref[...], preferred_element_type=jnp.float32)
    )
    left(HOME, 0)

    for q in range(CHUNKS):
        rows = pl.ds(q * step, step)
        held = parts[HOME, 0, rows]
        for t in range(PEERS):
            quarter_copy(t, q).wait_recv()
            held = pick(owners[t], parts[t, 0, rows], held)
        best[rows] = held
        cross_copy(q).start()
    for t in range(PEERS):
        forward_copy(t).start()
    for t in range(PEERS):
        left(t, 0)
    for t in (HOME, *range(PEERS)):
        forward_copy(t).wait_recv()
        left(t, 1)

    for q in range(CHUNKS):
        rows = pl.ds(q * step, step)
        cross_copy(q).wait_recv()
        chosen = pick(own_quad, best[rows], cross[rows])
        first = win * width + core * local_rows + q * step
        for r, e in enumerate(edge(chosen, w_r_ref[...], first)):
            right_ref[:, q * step + r, :] = e

    def contract(t, k):
        sums = [jnp.zeros((local_rows, channels), jnp.float32)] * local_rows
        for d in range(depth):
            right = right_ref[d]
            for r in range(local_rows):
                row = jnp.broadcast_to(left_ref[t, k, r, pl.ds(d, 1), :], (local_rows, channels))
                sums[r] = sums[r] + row * right
        return sums

    for t in range(PEERS + 1):
        for k in (1, 0):
            sums = contract(t, k)
            if (t, k) != (HOME, 0):
                for r in range(local_rows):
                    outbox[t, k, r] = sums[r].astype(jnp.bfloat16)
                partial_copy(t, k).start()

    here = list(sums)
    there = [jnp.zeros((local_rows, channels), jnp.float32)] * local_rows
    for t in range(PEERS + 1):
        for k in (1, 0):
            if (t, k) != (HOME, 0):
                partial_copy(t, k).wait_recv()
                for r in range(local_rows):
                    term = inbox[t, k, r].astype(jnp.float32)
                    if k == 0:
                        here[r] = here[r] + term
                    else:
                        there[r] = there[r] + term
    first_core = jnp.full((local_rows, channels), core, jnp.int32) == 0
    product = jnp.concatenate(
        [
            v
            for r in range(local_rows)
            for v in (jnp.where(first_core, here[r], there[r]), jnp.where(first_core, there[r], here[r]))
        ],
        axis=0,
    )
    normed_out = layer_norm(product, out_gain_ref[...]).astype(jnp.bfloat16)
    result = jnp.dot(normed_out, w_out_ref[...], preferred_element_type=jnp.float32)
    o_ref[...] = (gate_vals * result).astype(jnp.bfloat16).reshape(local_rows, width, channels)

    for q in range(CHUNKS):
        for t in range(PEERS):
            quarter_copy(t, q).wait_send()
        cross_copy(q).wait_send()
    for t in range(PEERS + 1):
        forward_copy(t).wait_send()
        for k in (1, 0):
            if (t, k) != (HOME, 0):
                partial_copy(t, k).wait_send()


def fused(
    pair_rows, in_gain, w_left, w_left_gate, w_right, w_right_gate, w_gate, w_out, out_gain, valid_len, window
):
    local_rows, tokens, channels = pair_rows.shape
    width = tokens // 8
    depth = tokens // QUAD
    part = (local_rows, depth, channels)
    mail = (QUAD, 2, local_rows, local_rows, channels)
    return pl.pallas_call(
        fused_kernel,
        out_shape=jax.ShapeDtypeStruct((local_rows, width, channels), jnp.bfloat16),
        in_specs=[pl.BlockSpec(memory_space=pltpu.HBM)] * 11,
        out_specs=pl.BlockSpec(memory_space=pltpu.VMEM),
        scratch_shapes=[
            pltpu.SMEM((1, 1), jnp.int32),
            pltpu.SMEM((1, 1), jnp.int32),
            pltpu.VMEM((local_rows, tokens, channels), jnp.bfloat16),
            pltpu.VMEM((1, channels), jnp.float32),
            pltpu.VMEM((channels, 2 * channels), jnp.bfloat16),
            pltpu.VMEM((channels, 2 * channels), jnp.bfloat16),
            pltpu.VMEM((channels, channels), jnp.bfloat16),
            pltpu.VMEM((channels, channels), jnp.bfloat16),
            pltpu.VMEM((1, channels), jnp.float32),
            pltpu.VMEM((QUAD, 2, *part), jnp.bfloat16),
            pltpu.VMEM(part, jnp.bfloat16),
            pltpu.VMEM(part, jnp.bfloat16),
            pltpu.VMEM((QUAD, 2, *part), jnp.float32),
            pltpu.VMEM((depth, local_rows, channels), jnp.float32),
            pltpu.VMEM(mail, jnp.bfloat16),
            pltpu.VMEM(mail, jnp.bfloat16),
            pltpu.SemaphoreType.DMA((PARTIAL + QUAD, 2)),
            pltpu.SemaphoreType.DMA((PARTIAL + QUAD, 2)),
            pltpu.SemaphoreType.DMA((12,)),
        ],
        compiler_params=pltpu.CompilerParams(collective_id=0, has_side_effects=True),
    )(
        valid_len.reshape(1, 1),
        window.reshape(1, 1),
        pair_rows,
        in_gain.reshape(1, channels),
        w_left,
        w_left_gate,
        w_right,
        w_right_gate,
        w_gate,
        w_out,
        out_gain.reshape(1, channels),
    )


def on_device_any(row_devices, pair_rows, *rest):
    local_rows, tokens, channels = pair_rows.shape
    fits = row_devices == QUAD * 4 and tokens // 8 == 2 * local_rows and local_rows % CHUNKS == 0
    return (fused if fits else on_device)(pair_rows, *rest)


def solution(mesh):
    return jax.shard_map(
        functools.partial(on_device_any, mesh.shape["row"]),
        mesh=mesh,
        in_specs=(
            P(("groups", "row"), None, None),
            P(),
            P(),
            P(),
            P(),
            P(),
            P(),
            P(),
            P(),
            P("groups"),
            P("groups"),
        ),
        out_specs=P(("groups", "row"), None, None),
        check_vma=False,
    )
```

```python
import functools

import jax
import jax.numpy as jnp
from jax import lax
from jax.experimental import pallas as pl
from jax.experimental.pallas import tpu as pltpu
from jax.sharding import PartitionSpec as P


def layer_norm(values, gain):
    mean_v = jnp.mean(values, axis=-1, keepdims=True)
    centered = values - mean_v
    variance_v = jnp.mean(centered * centered, axis=-1, keepdims=True)
    return centered * lax.rsqrt(variance_v + 1e-05) * gain


def on_device(
    pair_rows,
    in_gain,
    w_left,
    w_left_gate,
    w_right,
    w_right_gate,
    w_gate,
    w_out,
    out_gain,
    valid_len,
    window,
):
    my_index = lax.axis_index("row")
    local_rows, tokens_all, channels = pair_rows.shape
    width_win = tokens_all // 8
    valid_upto = valid_len[0]
    start_block = window[0]
    start_row = start_block * width_win
    row_ids = my_index * local_rows + jnp.arange(local_rows, dtype=jnp.int32)
    row_live = (row_ids < valid_upto).astype(jnp.float32)
    col_live = (jnp.arange(tokens_all, dtype=jnp.int32) < valid_upto).astype(jnp.float32)
    live_mask = (row_live[:, None] * col_live[None, :])[:, :, None]
    normed = layer_norm(pair_rows.astype(jnp.float32), in_gain).astype(jnp.bfloat16)
    flat_rows = normed.reshape(-1, channels)
    joined = jnp.concatenate([w_left, w_left_gate, w_right, w_right_gate], axis=1)
    projected = jnp.dot(flat_rows, joined, preferred_element_type=jnp.float32)
    projected = projected.reshape(local_rows, tokens_all, 4 * channels)
    left_edge = (
        jax.nn.sigmoid(projected[:, :, channels : 2 * channels])
        * projected[:, :, :channels]
        * live_mask
    ).astype(jnp.bfloat16)
    right_edge = (
        jax.nn.sigmoid(projected[:, :, 3 * channels :])
        * projected[:, :, 2 * channels : 3 * channels]
        * live_mask
    ).astype(jnp.bfloat16)
    gate_in = lax.dynamic_slice_in_dim(normed, start_row, width_win, 1)
    gate_vals = jax.nn.sigmoid(
        jnp.dot(gate_in.reshape(-1, channels), w_gate, preferred_element_type=jnp.float32)
    )
    gate_vals = gate_vals.reshape(local_rows, width_win, channels)
    regrouped = lax.all_to_all(right_edge, "row", split_axis=1, concat_axis=0, tiled=True)
    picked = lax.dynamic_slice_in_dim(regrouped, start_row, width_win, 0)
    window_right = lax.all_gather(picked, "row", axis=1, tiled=True)
    product = jnp.einsum(
        "ikc,jkc->ijc", left_edge, window_right, preferred_element_type=jnp.float32
    )
    normed_out = layer_norm(product, out_gain).astype(jnp.bfloat16)
    result = jnp.dot(normed_out.reshape(-1, channels), w_out, preferred_element_type=jnp.float32)
    return (gate_vals * result.reshape(local_rows, width_win, channels)).astype(jnp.bfloat16)


MESH = pl.DeviceIdType.MESH
CHUNKS = 2
QUAD = 4
PEERS = 3
HOME = PEERS
QUARTER, CROSS, FORWARD, PARTIAL = 0, PEERS, PEERS + 1, 2 * PEERS + 2


def fused_kernel(
    valid_hbm,
    window_hbm,
    x_hbm,
    in_gain_hbm,
    w_left_hbm,
    w_left_gate_hbm,
    w_right_hbm,
    w_right_gate_hbm,
    w_gate_hbm,
    w_out_hbm,
    out_gain_hbm,
    o_ref,
    valid_ref,
    window_ref,
    x_ref,
    in_gain_ref,
    w_l_ref,
    w_r_ref,
    w_gate_ref,
    w_out_ref,
    out_gain_ref,
    parts,
    best,
    cross,
    left_ref,
    right_ref,
    outbox,
    inbox,
    send_sem,
    recv_sem,
    load_sem,
):
    local_rows, tokens, channels = x_ref.shape
    depth = tokens // QUAD
    width = o_ref.shape[1]
    step = local_rows // CHUNKS

    me = lax.axis_index("row")
    core = lax.rem(me, 2)
    chip = lax.div(me, 2)
    quad = lax.div(chip, QUAD)
    spot = lax.rem(chip, QUAD)
    y = lax.rem(spot, 2)
    z = lax.div(spot, 2)
    spots = ((1 - z) * 2 + 1 - y, (1 - z) * 2 + y, z * 2 + 1 - y, spot)

    def at(quad_, spot_, core_):
        return {"row": (quad_ * QUAD + spot_) * 2 + core_}

    cores = (core, 1 - core)
    cross_peer = at(1 - quad, spot, core)
    partner = at(quad, spot, 1 - core)

    def quarter(s):
        return pl.ds(pl.multiple_of(s * depth, depth), depth)

    mine = quarter(spot)

    def remote(src, dst, kind, q, dev):
        return pltpu.make_async_remote_copy(
            src_ref=src,
            dst_ref=dst,
            send_sem=send_sem.at[kind, q],
            recv_sem=recv_sem.at[kind, q],
            device_id=dev,
            device_id_type=MESH,
        )

    def quarter_copy(t, q):
        rows = pl.ds(q * step, step)
        return remote(x_hbm.at[rows, quarter(spots[t])], parts.at[t, 0, rows], QUARTER + t, q, at(quad, spots[t], core))

    def cross_copy(q):
        rows = pl.ds(q * step, step)
        return remote(best.at[rows], cross.at[rows], CROSS, q, cross_peer)

    def forward_copy(t):
        src = x_hbm.at[:, mine] if t == HOME else parts.at[t, 0]
        return remote(src, parts.at[t, 1], FORWARD + t, 0, partner)

    def partial_copy(t, k):
        return remote(outbox.at[t, k], inbox.at[t, k], PARTIAL + t, k, at(quad, spots[t], cores[k]))

    barrier = pltpu.get_barrier_semaphore()
    everyone = [cross_peer] + [at(quad, s, c) for s in spots for c in cores][:-2] + [partner]
    for peer in everyone:
        pl.semaphore_signal(barrier, inc=1, device_id=peer, device_id_type=MESH)
    half = pl.ds(0, channels)
    other = pl.ds(channels, channels)
    loads = [
        pltpu.make_async_copy(src, dst, load_sem.at[n])
        for n, (src, dst) in enumerate(
            (
                (x_hbm.at[:, mine], parts.at[HOME, 0]),
                (valid_hbm, valid_ref),
                (window_hbm, window_ref),
                (in_gain_hbm, in_gain_ref),
                (w_left_hbm, w_l_ref.at[:, half]),
                (w_left_gate_hbm, w_l_ref.at[:, other]),
                (x_hbm, x_ref),
                (w_gate_hbm, w_gate_ref),
                (w_right_hbm, w_r_ref.at[:, half]),
                (w_right_gate_hbm, w_r_ref.at[:, other]),
                (w_out_hbm, w_out_ref),
                (out_gain_hbm, out_gain_ref),
            )
        )
    ]
    for load in loads:
        load.start()
    pl.semaphore_wait(barrier, len(everyone))
    for q in range(CHUNKS):
        for t in range(PEERS):
            quarter_copy(t, q).start()
    forward_copy(HOME).start()
    for load in loads:
        load.wait()

    win = window_ref[0, 0]
    valid = valid_ref[0, 0]
    win_v = jnp.full((depth, channels), win, jnp.int32)

    def flag(cond):
        return jnp.where(cond, 1.0, 0.0).astype(jnp.bfloat16)

    owners = [flag(win_v == quad * QUAD + s) for s in spots[:PEERS]]
    own_quad = flag(jnp.logical_and(win_v >= quad * QUAD, win_v < (quad + 1) * QUAD))

    def pick(own, a, b):
        return jnp.where((own > 0)[None], a, b)

    gain = in_gain_ref[...]
    k_ids = spot * depth + lax.broadcasted_iota(jnp.int32, (depth, channels), 0)
    valid_v = jnp.full((depth, channels), valid, jnp.int32)
    k_live = k_ids < valid_v

    def normal(rows):
        flat = rows.astype(jnp.float32).reshape(-1, channels)
        return layer_norm(flat, gain).astype(jnp.bfloat16)

    def edge(rows, weights, first):
        count = rows.shape[0]
        proj = jnp.dot(normal(rows), weights, preferred_element_type=jnp.float32)
        val = jax.nn.sigmoid(proj[:, channels:]) * proj[:, :channels]
        val = val.reshape(count, depth, channels)
        row_v = jnp.full((depth, channels), first, jnp.int32)
        out = []
        for r in range(count):
            live = jnp.logical_and(k_live, row_v + r < valid_v)
            rounded = jnp.where(live, val[r], 0.0).astype(jnp.bfloat16)
            out.append(rounded.astype(jnp.float32))
        return out

    def left(t, k):
        first = ((quad * QUAD + spots[t]) * 2 + cores[k]) * local_rows
        for r, e in enumerate(edge(parts[t, k], w_l_ref[...], first)):
            left_ref[t, k, r] = e

    gate_in = x_ref[:, :width, :]
    for block in range(1, tokens // width):
        at_block = flag(win_v[:width] == block)
        gate_in = pick(at_block, x_ref[:, block * width : (block + 1) * width, :], gate_in)
    gate_in = normal(gate_in)
    gate_vals = jax.nn.sigmoid(
        jnp.dot(gate_in, w_gate_ref[...], preferred_element_type=jnp.float32)
    )
    left(HOME, 0)

    for q in range(CHUNKS):
        rows = pl.ds(q * step, step)
        held = parts[HOME, 0, rows]
        for t in range(PEERS):
            quarter_copy(t, q).wait_recv()
            held = pick(owners[t], parts[t, 0, rows], held)
        best[rows] = held
        cross_copy(q).start()
    for t in range(PEERS):
        forward_copy(t).start()
    for t in range(PEERS):
        left(t, 0)
    for t in (HOME, *range(PEERS)):
        forward_copy(t).wait_recv()
        left(t, 1)

    for q in range(CHUNKS):
        rows = pl.ds(q * step, step)
        cross_copy(q).wait_recv()
        chosen = pick(own_quad, best[rows], cross[rows])
        first = win * width + core * local_rows + q * step
        for r, e in enumerate(edge(chosen, w_r_ref[...], first)):
            right_ref[:, q * step + r, :] = e

    def contract(t, k):
        sums = [jnp.zeros((local_rows, channels), jnp.float32)] * local_rows
        for d in range(depth):
            right = right_ref[d]
            for r in range(local_rows):
                row = jnp.broadcast_to(left_ref[t, k, r, pl.ds(d, 1), :], (local_rows, channels))
                sums[r] = sums[r] + row * right
        return sums

    for t in range(PEERS + 1):
        for k in (1, 0):
            sums = contract(t, k)
            if (t, k) != (HOME, 0):
                for r in range(local_rows):
                    outbox[t, k, r] = sums[r].astype(jnp.bfloat16)
                partial_copy(t, k).start()

    here = list(sums)
    there = [jnp.zeros((local_rows, channels), jnp.float32)] * local_rows
    for t in range(PEERS + 1):
        for k in (1, 0):
            if (t, k) != (HOME, 0):
                partial_copy(t, k).wait_recv()
                for r in range(local_rows):
                    term = inbox[t, k, r].astype(jnp.float32)
                    if k == 0:
                        here[r] = here[r] + term
                    else:
                        there[r] = there[r] + term
    first_core = jnp.full((local_rows, channels), core, jnp.int32) == 0
    product = jnp.concatenate(
        [
            v
            for r in range(local_rows)
            for v in (jnp.where(first_core, here[r], there[r]), jnp.where(first_core, there[r], here[r]))
        ],
        axis=0,
    )
    normed_out = layer_norm(product, out_gain_ref[...]).astype(jnp.bfloat16)
    result = jnp.dot(normed_out, w_out_ref[...], preferred_element_type=jnp.float32)
    o_ref[...] = (gate_vals * result).astype(jnp.bfloat16).reshape(local_rows, width, channels)

    for q in range(CHUNKS):
        for t in range(PEERS):
            quarter_copy(t, q).wait_send()
        cross_copy(q).wait_send()
    for t in range(PEERS + 1):
        forward_copy(t).wait_send()
        for k in (1, 0):
            if (t, k) != (HOME, 0):
                partial_copy(t, k).wait_send()


def fused(
    pair_rows, in_gain, w_left, w_left_gate, w_right, w_right_gate, w_gate, w_out, out_gain, valid_len, window
):
    local_rows, tokens, channels = pair_rows.shape
    width = tokens // 8
    depth = tokens // QUAD
    part = (local_rows, depth, channels)
    mail = (QUAD, 2, local_rows, local_rows, channels)
    return pl.pallas_call(
        fused_kernel,
        out_shape=pltpu.VMEM((local_rows, width, channels), jnp.bfloat16),
        in_specs=[pl.BlockSpec(memory_space=pltpu.HBM)] * 11,
        out_specs=pl.BlockSpec(memory_space=pltpu.VMEM),
        scratch_shapes=[
            pltpu.SMEM((1, 1), jnp.int32),
            pltpu.SMEM((1, 1), jnp.int32),
            pltpu.VMEM((local_rows, tokens, channels), jnp.bfloat16),
            pltpu.VMEM((1, channels), jnp.float32),
            pltpu.VMEM((channels, 2 * channels), jnp.bfloat16),
            pltpu.VMEM((channels, 2 * channels), jnp.bfloat16),
            pltpu.VMEM((channels, channels), jnp.bfloat16),
            pltpu.VMEM((channels, channels), jnp.bfloat16),
            pltpu.VMEM((1, channels), jnp.float32),
            pltpu.VMEM((QUAD, 2, *part), jnp.bfloat16),
            pltpu.VMEM(part, jnp.bfloat16),
            pltpu.VMEM(part, jnp.bfloat16),
            pltpu.VMEM((QUAD, 2, *part), jnp.float32),
            pltpu.VMEM((depth, local_rows, channels), jnp.float32),
            pltpu.VMEM(mail, jnp.bfloat16),
            pltpu.VMEM(mail, jnp.bfloat16),
            pltpu.SemaphoreType.DMA((PARTIAL + QUAD, 2)),
            pltpu.SemaphoreType.DMA((PARTIAL + QUAD, 2)),
            pltpu.SemaphoreType.DMA((12,)),
        ],
        compiler_params=pltpu.CompilerParams(collective_id=0, has_side_effects=True),
    )(
        valid_len.reshape(1, 1),
        window.reshape(1, 1),
        pair_rows,
        in_gain.reshape(1, channels),
        w_left,
        w_left_gate,
        w_right,
        w_right_gate,
        w_gate,
        w_out,
        out_gain.reshape(1, channels),
    )


def on_device_any(row_devices, pair_rows, *rest):
    local_rows, tokens, channels = pair_rows.shape
    fits = row_devices == QUAD * 4 and tokens // 8 == 2 * local_rows and local_rows % CHUNKS == 0
    return (fused if fits else on_device)(pair_rows, *rest)


def solution(mesh):
    return jax.shard_map(
        functools.partial(on_device_any, mesh.shape["row"]),
        mesh=mesh,
        in_specs=(
            P(("groups", "row"), None, None),
            P(),
            P(),
            P(),
            P(),
            P(),
            P(),
            P(),
            P(),
            P("groups"),
            P("groups"),
        ),
        out_specs=P(("groups", "row"), None, None),
        check_vma=False,
    )
```

```python
import functools

import jax
import jax.numpy as jnp
from jax import lax
from jax.experimental import pallas as pl
from jax.experimental.pallas import tpu as pltpu
from jax.sharding import PartitionSpec as P


def layer_norm(values, gain):
    mean_v = jnp.mean(values, axis=-1, keepdims=True)
    centered = values - mean_v
    variance_v = jnp.mean(centered * centered, axis=-1, keepdims=True)
    return centered * lax.rsqrt(variance_v + 1e-05) * gain


def on_device(
    pair_rows,
    in_gain,
    w_left,
    w_left_gate,
    w_right,
    w_right_gate,
    w_gate,
    w_out,
    out_gain,
    valid_len,
    window,
):
    my_index = lax.axis_index("row")
    local_rows, tokens_all, channels = pair_rows.shape
    width_win = tokens_all // 8
    valid_upto = valid_len[0]
    start_block = window[0]
    start_row = start_block * width_win
    row_ids = my_index * local_rows + jnp.arange(local_rows, dtype=jnp.int32)
    row_live = (row_ids < valid_upto).astype(jnp.float32)
    col_live = (jnp.arange(tokens_all, dtype=jnp.int32) < valid_upto).astype(jnp.float32)
    live_mask = (row_live[:, None] * col_live[None, :])[:, :, None]
    normed = layer_norm(pair_rows.astype(jnp.float32), in_gain).astype(jnp.bfloat16)
    flat_rows = normed.reshape(-1, channels)
    joined = jnp.concatenate([w_left, w_left_gate, w_right, w_right_gate], axis=1)
    projected = jnp.dot(flat_rows, joined, preferred_element_type=jnp.float32)
    projected = projected.reshape(local_rows, tokens_all, 4 * channels)
    left_edge = (
        jax.nn.sigmoid(projected[:, :, channels : 2 * channels])
        * projected[:, :, :channels]
        * live_mask
    ).astype(jnp.bfloat16)
    right_edge = (
        jax.nn.sigmoid(projected[:, :, 3 * channels :])
        * projected[:, :, 2 * channels : 3 * channels]
        * live_mask
    ).astype(jnp.bfloat16)
    gate_in = lax.dynamic_slice_in_dim(normed, start_row, width_win, 1)
    gate_vals = jax.nn.sigmoid(
        jnp.dot(gate_in.reshape(-1, channels), w_gate, preferred_element_type=jnp.float32)
    )
    gate_vals = gate_vals.reshape(local_rows, width_win, channels)
    regrouped = lax.all_to_all(right_edge, "row", split_axis=1, concat_axis=0, tiled=True)
    picked = lax.dynamic_slice_in_dim(regrouped, start_row, width_win, 0)
    window_right = lax.all_gather(picked, "row", axis=1, tiled=True)
    product = jnp.einsum(
        "ikc,jkc->ijc", left_edge, window_right, preferred_element_type=jnp.float32
    )
    normed_out = layer_norm(product, out_gain).astype(jnp.bfloat16)
    result = jnp.dot(normed_out.reshape(-1, channels), w_out, preferred_element_type=jnp.float32)
    return (gate_vals * result.reshape(local_rows, width_win, channels)).astype(jnp.bfloat16)


MESH = pl.DeviceIdType.MESH
CHUNKS = 2
QUAD = 4
PEERS = 3
HOME = PEERS
QUARTER, CROSS, FORWARD, PARTIAL = 0, PEERS, PEERS + 1, 2 * PEERS + 2


def fused_kernel(
    valid_hbm,
    window_hbm,
    x_hbm,
    in_gain_hbm,
    w_left_hbm,
    w_left_gate_hbm,
    w_right_hbm,
    w_right_gate_hbm,
    w_gate_hbm,
    w_out_hbm,
    out_gain_hbm,
    o_ref,
    valid_ref,
    window_ref,
    x_ref,
    in_gain_ref,
    w_l_ref,
    w_r_ref,
    w_gate_ref,
    w_out_ref,
    out_gain_ref,
    parts,
    best,
    cross,
    left_ref,
    right_ref,
    outbox,
    inbox,
    send_sem,
    recv_sem,
    load_sem,
):
    local_rows, tokens, channels = x_ref.shape
    depth = tokens // QUAD
    width = o_ref.shape[1]
    step = local_rows // CHUNKS

    me = lax.axis_index("row")
    core = lax.rem(me, 2)
    chip = lax.div(me, 2)
    quad = lax.div(chip, QUAD)
    spot = lax.rem(chip, QUAD)
    y = lax.rem(spot, 2)
    z = lax.div(spot, 2)
    spots = ((1 - z) * 2 + 1 - y, (1 - z) * 2 + y, z * 2 + 1 - y, spot)

    def at(quad_, spot_, core_):
        return {"row": (quad_ * QUAD + spot_) * 2 + core_}

    cores = (core, 1 - core)
    cross_peer = at(1 - quad, spot, core)
    partner = at(quad, spot, 1 - core)

    def quarter(s):
        return pl.ds(pl.multiple_of(s * depth, depth), depth)

    mine = quarter(spot)

    def remote(src, dst, kind, q, dev):
        return pltpu.make_async_remote_copy(
            src_ref=src,
            dst_ref=dst,
            send_sem=send_sem.at[kind, q],
            recv_sem=recv_sem.at[kind, q],
            device_id=dev,
            device_id_type=MESH,
        )

    def quarter_copy(t, q):
        rows = pl.ds(q * step, step)
        return remote(x_hbm.at[rows, quarter(spots[t])], parts.at[t, 0, rows], QUARTER + t, q, at(quad, spots[t], core))

    def cross_copy(q):
        rows = pl.ds(q * step, step)
        return remote(best.at[rows], cross.at[rows], CROSS, q, cross_peer)

    def forward_copy(t):
        src = x_hbm.at[:, mine] if t == HOME else parts.at[t, 0]
        return remote(src, parts.at[t, 1], FORWARD + t, 0, partner)

    def partial_copy(t, k):
        return remote(outbox.at[t, k], inbox.at[t, k], PARTIAL + t, k, at(quad, spots[t], cores[k]))

    barrier = pltpu.get_barrier_semaphore()
    everyone = [cross_peer] + [at(quad, s, core) for s in spots[:PEERS]] + [partner]
    for peer in everyone:
        pl.semaphore_signal(barrier, inc=1, device_id=peer, device_id_type=MESH)
    half = pl.ds(0, channels)
    other = pl.ds(channels, channels)
    loads = [
        pltpu.make_async_copy(src, dst, load_sem.at[n])
        for n, (src, dst) in enumerate(
            (
                (x_hbm.at[:, mine], parts.at[HOME, 0]),
                (valid_hbm, valid_ref),
                (window_hbm, window_ref),
                (in_gain_hbm, in_gain_ref),
                (w_left_hbm, w_l_ref.at[:, half]),
                (w_left_gate_hbm, w_l_ref.at[:, other]),
                (x_hbm, x_ref),
                (w_gate_hbm, w_gate_ref),
                (w_right_hbm, w_r_ref.at[:, half]),
                (w_right_gate_hbm, w_r_ref.at[:, other]),
                (w_out_hbm, w_out_ref),
                (out_gain_hbm, out_gain_ref),
            )
        )
    ]
    pl.semaphore_wait(barrier, len(everyone))
    for q in range(CHUNKS):
        for t in range(PEERS):
            quarter_copy(t, q).start()
    for load in loads:
        load.start()
    forward_copy(HOME).start()
    for load in loads:
        load.wait()

    win = window_ref[0, 0]
    valid = valid_ref[0, 0]
    win_v = jnp.full((depth, channels), win, jnp.int32)

    def flag(cond):
        return jnp.where(cond, 1.0, 0.0).astype(jnp.bfloat16)

    owners = [flag(win_v == quad * QUAD + s) for s in spots[:PEERS]]
    own_quad = flag(jnp.logical_and(win_v >= quad * QUAD, win_v < (quad + 1) * QUAD))

    def pick(own, a, b):
        return jnp.where((own > 0)[None], a, b)

    gain = in_gain_ref[...]
    k_ids = spot * depth + lax.broadcasted_iota(jnp.int32, (depth, channels), 0)
    valid_v = jnp.full((depth, channels), valid, jnp.int32)
    k_live = k_ids < valid_v

    def normal(rows):
        flat = rows.astype(jnp.float32).reshape(-1, channels)
        return layer_norm(flat, gain).astype(jnp.bfloat16)

    def edge(rows, weights, first):
        count = rows.shape[0]
        proj = jnp.dot(normal(rows), weights, preferred_element_type=jnp.float32)
        val = jax.nn.sigmoid(proj[:, channels:]) * proj[:, :channels]
        val = val.reshape(count, depth, channels)
        row_v = jnp.full((depth, channels), first, jnp.int32)
        out = []
        for r in range(count):
            live = jnp.logical_and(k_live, row_v + r < valid_v)
            rounded = jnp.where(live, val[r], 0.0).astype(jnp.bfloat16)
            out.append(rounded.astype(jnp.float32))
        return out

    def left(t, k):
        first = ((quad * QUAD + spots[t]) * 2 + cores[k]) * local_rows
        for r, e in enumerate(edge(parts[t, k], w_l_ref[...], first)):
            left_ref[t, k, r] = e

    for q in range(CHUNKS):
        rows = pl.ds(q * step, step)
        held = parts[HOME, 0, rows]
        for t in range(PEERS):
            quarter_copy(t, q).wait_recv()
            held = pick(owners[t], parts[t, 0, rows], held)
        best[rows] = held
        cross_copy(q).start()
    gate_in = x_ref[:, :width, :]
    for block in range(1, tokens // width):
        at_block = flag(win_v[:width] == block)
        gate_in = pick(at_block, x_ref[:, block * width : (block + 1) * width, :], gate_in)
    gate_in = normal(gate_in)
    gate_vals = jax.nn.sigmoid(
        jnp.dot(gate_in, w_gate_ref[...], preferred_element_type=jnp.float32)
    )
    left(HOME, 0)

    for t in range(PEERS):
        forward_copy(t).start()
    for t in range(PEERS):
        left(t, 0)
    for t in (HOME, *range(PEERS)):
        forward_copy(t).wait_recv()
        left(t, 1)

    for q in range(CHUNKS):
        rows = pl.ds(q * step, step)
        cross_copy(q).wait_recv()
        chosen = pick(own_quad, best[rows], cross[rows])
        first = win * width + core * local_rows + q * step
        for r, e in enumerate(edge(chosen, w_r_ref[...], first)):
            right_ref[:, q * step + r, :] = e

    def contract(t, k):
        sums = [jnp.zeros((local_rows, channels), jnp.float32)] * local_rows
        for d in range(depth):
            right = right_ref[d]
            for r in range(local_rows):
                row = jnp.broadcast_to(left_ref[t, k, r, pl.ds(d, 1), :], (local_rows, channels))
                sums[r] = sums[r] + row * right
        return sums

    for t in range(PEERS + 1):
        for k in (1, 0):
            sums = contract(t, k)
            if (t, k) != (HOME, 0):
                for r in range(local_rows):
                    outbox[t, k, r] = sums[r].astype(jnp.bfloat16)
                partial_copy(t, k).start()

    here = list(sums)
    there = [jnp.zeros((local_rows, channels), jnp.float32)] * local_rows
    for t in range(PEERS + 1):
        for k in (1, 0):
            if (t, k) != (HOME, 0):
                partial_copy(t, k).wait_recv()
                for r in range(local_rows):
                    term = inbox[t, k, r].astype(jnp.float32)
                    if k == 0:
                        here[r] = here[r] + term
                    else:
                        there[r] = there[r] + term
    first_core = jnp.full((local_rows, channels), core, jnp.int32) == 0
    product = jnp.concatenate(
        [
            v
            for r in range(local_rows)
            for v in (jnp.where(first_core, here[r], there[r]), jnp.where(first_core, there[r], here[r]))
        ],
        axis=0,
    )
    normed_out = layer_norm(product, out_gain_ref[...]).astype(jnp.bfloat16)
    result = jnp.dot(normed_out, w_out_ref[...], preferred_element_type=jnp.float32)
    o_ref[...] = (gate_vals * result).astype(jnp.bfloat16).reshape(local_rows, width, channels)

    for q in range(CHUNKS):
        for t in range(PEERS):
            quarter_copy(t, q).wait_send()
        cross_copy(q).wait_send()
    for t in range(PEERS + 1):
        forward_copy(t).wait_send()
        for k in (1, 0):
            if (t, k) != (HOME, 0):
                partial_copy(t, k).wait_send()


def fused(
    pair_rows, in_gain, w_left, w_left_gate, w_right, w_right_gate, w_gate, w_out, out_gain, valid_len, window
):
    local_rows, tokens, channels = pair_rows.shape
    width = tokens // 8
    depth = tokens // QUAD
    part = (local_rows, depth, channels)
    mail = (QUAD, 2, local_rows, local_rows, channels)
    return pl.pallas_call(
        fused_kernel,
        out_shape=pltpu.VMEM((local_rows, width, channels), jnp.bfloat16),
        in_specs=[pl.BlockSpec(memory_space=pltpu.HBM)] * 11,
        out_specs=pl.BlockSpec(memory_space=pltpu.VMEM),
        scratch_shapes=[
            pltpu.SMEM((1, 1), jnp.int32),
            pltpu.SMEM((1, 1), jnp.int32),
            pltpu.VMEM((local_rows, tokens, channels), jnp.bfloat16),
            pltpu.VMEM((1, channels), jnp.float32),
            pltpu.VMEM((channels, 2 * channels), jnp.bfloat16),
            pltpu.VMEM((channels, 2 * channels), jnp.bfloat16),
            pltpu.VMEM((channels, channels), jnp.bfloat16),
            pltpu.VMEM((channels, channels), jnp.bfloat16),
            pltpu.VMEM((1, channels), jnp.float32),
            pltpu.VMEM((QUAD, 2, *part), jnp.bfloat16),
            pltpu.VMEM(part, jnp.bfloat16),
            pltpu.VMEM(part, jnp.bfloat16),
            pltpu.VMEM((QUAD, 2, *part), jnp.float32),
            pltpu.VMEM((depth, local_rows, channels), jnp.float32),
            pltpu.VMEM(mail, jnp.bfloat16),
            pltpu.VMEM(mail, jnp.bfloat16),
            pltpu.SemaphoreType.DMA((PARTIAL + QUAD, 2)),
            pltpu.SemaphoreType.DMA((PARTIAL + QUAD, 2)),
            pltpu.SemaphoreType.DMA((12,)),
        ],
        compiler_params=pltpu.CompilerParams(collective_id=0, has_side_effects=True),
    )(
        valid_len.reshape(1, 1),
        window.reshape(1, 1),
        pair_rows,
        in_gain.reshape(1, channels),
        w_left,
        w_left_gate,
        w_right,
        w_right_gate,
        w_gate,
        w_out,
        out_gain.reshape(1, channels),
    )


def on_device_any(row_devices, pair_rows, *rest):
    local_rows, tokens, channels = pair_rows.shape
    fits = row_devices == QUAD * 4 and tokens // 8 == 2 * local_rows and local_rows % CHUNKS == 0
    return (fused if fits else on_device)(pair_rows, *rest)


def solution(mesh):
    return jax.shard_map(
        functools.partial(on_device_any, mesh.shape["row"]),
        mesh=mesh,
        in_specs=(
            P(("groups", "row"), None, None),
            P(),
            P(),
            P(),
            P(),
            P(),
            P(),
            P(),
            P(),
            P("groups"),
            P("groups"),
        ),
        out_specs=P(("groups", "row"), None, None),
        check_vma=False,
    )
```
